128 devices in a mesh: row: 8 (over y_lo, x), col: 8 (over y_hi, z), depth: 2 (over core).
Axes of the slice: x: 4, y: 4 (y_hi: 2, y_lo: 2; y = y_hi * 2 + y_lo), z: 4, core: 2. Of those that a mesh axis runs over, the one named last changes fastest.
Arguments:
- x_blocks: float32 [96, 32, 128, 128], P(('row', 'depth'), 'col'), may hold values from -1.2 to 1.2
- x_cols: int32 [96, 32], P(('row', 'depth'), 'col'), may hold values from 0 to 11, as said below
- c_cols: int32 [96, 32], P(('row', 'depth'), 'col'), may hold values from 0 to 11, as said below
Outputs:
- c_blocks: float32 [96, 32, 128, 128], P(('row', 'depth'), 'col')
The draws below stay inside these ranges and needn't reach their ends.
Inputs may be any that keep to these rules, and one draw needn't show every extreme that they name: `x_cols`: within one block row and column tile the 4 entries are distinct. `c_cols`: within one block row and column tile the 4 entries are distinct.
All inputs are finite; a program needn't handle non-finite values.
Results may differ from the reference program's by a relative error of at most 0.0003.
Values sent between devices are 32-bit elements; how exact they have to be, the bound alone decides.
No kernel may reach another device: no remote copies, remote signals or barrier semaphores. Data moves between devices by JAX's collectives and lax.ppermute only.
A program may use at most 128 MiB of HBM per device.

```python
import jax
import jax.numpy as jnp
from jax import lax

BS = 128
SLOTS = 4
OUT_SLOTS = 4
NB = 96
TILE = 12
N_COL = 8


def distinct_columns(key, count):
    scores = jax.random.randint(key, (NB, N_COL, TILE), 0, 1 << 20, dtype=jnp.int32)
    scores = scores * TILE + jnp.arange(TILE, dtype=jnp.int32)
    order = jnp.argsort(scores, axis=-1)[:, :, :count]
    return order.astype(jnp.int32).reshape(NB, N_COL * count)


def draw_x_cols(key, part):
    return distinct_columns(jax.random.fold_in(key, 11), SLOTS)


def draw_c_cols(key, part):
    return distinct_columns(jax.random.fold_in(key, 23), OUT_SLOTS)


def block_levels(rng, extent, cuts, low, high):
    gain, own = 1.0, jax.random.fold_in(rng, 6)
    for dim, shards_of in cuts:
        heights = jnp.exp(jax.random.uniform(jax.random.fold_in(own, dim), (shards_of,), jnp.float32, low / len(cuts), high / len(cuts)))
        gain = gain * jnp.repeat(heights, extent[dim] // shards_of).reshape([-1 if axis == dim else 1 for axis in range(len(extent))])
    return gain


def bell_draw(rng, shape, deviation, bound, shards=(), held_as=jnp.bfloat16):
    array = jax.random.normal(rng, shape, jnp.float32) * deviation
    if len(shards) > 0:
        array = block_levels(rng, shape, shards, -0.22, 0.18) * array
    return jnp.clip(array, min=-bound, max=bound).astype(held_as)


def setup_inputs(seed: int = 0) -> dict:
    key_list = jax.random.split(jax.random.key(seed), 4)
    x_blocks = bell_draw(key_list[0], (NB, N_COL * SLOTS, BS, BS), 0.2, 1.2, ((0, 16), (1, 8)), jnp.float32)
    x_cols = draw_x_cols(jax.random.fold_in(key_list[3], 71), 0)
    c_cols = draw_c_cols(jax.random.fold_in(key_list[3], 71), 0)
    return {"x_blocks": x_blocks, "x_cols": x_cols, "c_cols": c_cols}


def block_product(left_blocks, left_cols, right_blocks, right_cols, out_cols):
    picked = jnp.take(right_blocks, left_cols, axis=0)
    picked_cols = jnp.take(right_cols, left_cols, axis=0)
    partial_prod = jnp.einsum("isab,istbc->istac", left_blocks, picked, precision=lax.Precision.HIGHEST)
    matches = (picked_cols[:, :, :, None] == out_cols[:, None, None, :]).astype(jnp.float32)
    return jnp.einsum("istu,istac->iuac", matches, partial_prod, precision=lax.Precision.HIGHEST)


def reference(x_blocks, x_cols, c_cols):
    blocks = x_blocks.reshape(NB, N_COL, SLOTS, BS, BS)
    columns = x_cols.reshape(NB, N_COL, SLOTS)
    kept = c_cols.reshape(NB, N_COL, OUT_SLOTS)

    def one_tile(column_tile):
        kept_here = lax.dynamic_index_in_dim(kept, column_tile, 1, keepdims=False)
        right_all = lax.dynamic_index_in_dim(blocks, column_tile, 1, keepdims=False)
        right_cols_all = lax.dynamic_index_in_dim(columns, column_tile, 1, keepdims=False)

        def add_panel(inner, accum):
            left_here = lax.dynamic_index_in_dim(blocks, inner, 1, keepdims=False)
            left_cols = lax.dynamic_index_in_dim(columns, inner, 1, keepdims=False)
            start = (inner * TILE).astype(jnp.int32)
            right_here = lax.dynamic_slice_in_dim(right_all, start, TILE, 0)
            right_cols = lax.dynamic_slice_in_dim(right_cols_all, start, TILE, 0)
            return accum + block_product(left_here, left_cols, right_here, right_cols, kept_here)

        initial = jnp.zeros((NB, OUT_SLOTS, BS, BS), jnp.float32)
        return lax.fori_loop(0, N_COL, add_panel, initial)

    result = lax.map(one_tile, jnp.arange(N_COL, dtype=jnp.int32))
    return jnp.transpose(result, (1, 0, 2, 3, 4)).reshape(NB, N_COL * OUT_SLOTS, BS, BS)
```

```python
import functools

import jax
import jax.numpy as jnp
import numpy as np
from jax import lax
from jax.experimental import pallas as pl
from jax.experimental.pallas import tpu as pltpu
from jax.sharding import PartitionSpec as P


AXES = ("row", "col", "depth")
RING = 4
HALF = 6
SLOTS = 4
BS = 128
ROWS = HALF * SLOTS * BS
EXTRA = 8
GROUP = 8
TRASH = HALF * SLOTS
F32, BF16 = jnp.float32, jnp.bfloat16


def device_number(x, y, z, d):
    y_hi, y_lo = y >> 1, y & 1
    return (y_lo * RING + x) * 16 + (y_hi * RING + z) * 2 + d


def all_places():
    return [(x, y, z, d) for x in range(4) for y in range(4) for z in range(4) for d in range(2)]


def move(value, dx=0, dz=0, y_flip=0, d_flip=0):
    pairs = [
        (
            device_number(x, y, z, d),
            device_number((x + dx) % 4, y ^ y_flip, (z + dz) % 4, d ^ d_flip),
        )
        for x, y, z, d in all_places()
    ]
    return lax.ppermute(value, AXES, pairs)


STAGE = (0, 0, 0, 0, 0, 1, 1, 2)


def panel_table():
    table = np.zeros((128, 3, 17), np.int32)
    for x, y, z, d in all_places():
        rows = table[device_number(x, y, z, d)]
        for h in range(2):
            for w in range(4):
                left = 4 * (h != y >> 1) + (0, 2, 3, 1)[(w - z) % 4]
                right = 4 * (h != (y & 1)) + (0, 2, 3, 1)[(w - x) % 4]
                row = rows[max(STAGE[left], STAGE[right])]
                row[1 + 2 * row[0]] = left
                row[2 + 2 * row[0]] = right
                row[0] += 1
    return table


def split(value):
    high = value.astype(BF16)
    return high, (value - high.astype(F32)).astype(BF16)


def product(a, b):
    a_high, a_low = split(a)
    b_high, b_low = split(b)
    side = jnp.concatenate([b_high, b_low], 1)
    both = jnp.dot(
        jnp.concatenate([a_high, a_low], 1),
        jnp.concatenate([side, side], 0),
        preferred_element_type=F32,
    )
    return both[:, :BS] + both[:, BS:]


def gate_kernel(a_ref, o_ref):
    for i in range(3):
        for j in range(17):
            o_ref[i, j] = a_ref[i, j]


def gate(meta):
    return pl.pallas_call(
        gate_kernel,
        out_shape=jax.ShapeDtypeStruct((3, 17), jnp.int32),
        in_specs=[pl.BlockSpec(memory_space=pltpu.SMEM)],
        out_specs=pl.BlockSpec(memory_space=pltpu.SMEM),
        cost_estimate=pl.CostEstimate(flops=100, bytes_accessed=1000, transcendentals=0),
    )(meta)


def panels_kernel(stage, lefts, rights, first, n_refs, depth_ref, meta_ref, kept_ref, *refs):
    pieces = refs[:n_refs]
    at = n_refs
    before = None
    if not first:
        before = refs[at]
        at += 1
    out, lb, rb, cb, lc, rc, inv, lst, sem, csem = refs[at:]
    depth = depth_ref[0]
    count = meta_ref[stage, 0]
    whole = pl.ds(0, ROWS)

    def copies(j, sources, dst, cols, data_sem, col_sem):
        for ref, src, rows, to, has_cols in sources[j]:
            pltpu.make_async_copy(
                pieces[ref].at[pl.ds(src, rows)], dst.at[pl.ds(to, rows)], data_sem
            ).start()
            if has_cols:
                pltpu.make_async_copy(
                    pieces[ref].at[pl.ds(src + rows, EXTRA)], cols, col_sem
                ).start()

    def fetch(n, slot):
        left, right = meta_ref[stage, 1 + 2 * n], meta_ref[stage, 2 + 2 * n]
        for j in lefts:
            @pl.when(left == j)
            def _():
                copies(j, lefts, lb.at[slot], lc.at[slot], sem.at[slot, 0], csem.at[slot, 0])
        for j in rights:
            @pl.when(right == j)
            def _():
                for mine in range(2):
                    half = depth if mine == 0 else 1 - depth
                    copies(
                        (j, mine),
                        rights[j],
                        rb.at[slot, pl.ds(pl.multiple_of(half * ROWS, ROWS), ROWS)],
                        rc.at[slot, half],
                        sem.at[slot, 1 + mine],
                        csem.at[slot, 1 + mine],
                    )

    @pl.when(count > 0)
    def _():
        fetch(0, 0)

    if first:
        cb[...] = jnp.zeros_like(cb)
    else:
        load = pltpu.make_async_copy(before, cb.at[whole], sem.at[0, 3])
        load.start()

    def clear(n, carry):
        inv[n] = -1
        return carry

    lax.fori_loop(0, HALF * 16, clear, 0)
    for i in range(HALF):
        for u in range(SLOTS):
            inv[i * 16 + kept_ref[i, u]] = u
    if not first:
        load.wait()

    def panel(n, carry):
        slot = lax.rem(n, 2)

        @pl.when(n + 1 < count)
        def _():
            fetch(n + 1, 1 - slot)

        pltpu.make_async_copy(lc.at[slot], lc.at[slot], csem.at[slot, 0]).wait()
        for mine in range(2):
            pltpu.make_async_copy(rc.at[slot, 0], rc.at[slot, 0], csem.at[slot, 1 + mine]).wait()

        def list_row(e, total):
            i = e // SLOTS
            k = lc[slot, 0, e].astype(jnp.int32)
            half = (k >= HALF).astype(jnp.int32)
            base = (k - HALF * half) * SLOTS
            code = e + k * 256
            for t in range(SLOTS):
                column = rc[slot, half, 0, base + t].astype(jnp.int32)
                u = inv[i * 16 + column]
                lst[total] = code + t * 64 + (i * SLOTS + u) * 4096
                total = total + (u >= 0).astype(jnp.int32)
            return total

        total = lax.fori_loop(0, HALF * SLOTS, list_row, 0)
        for q in range(GROUP):
            lst[total + q] = TRASH * 4096
        pltpu.make_async_copy(lb.at[slot], lb.at[slot], sem.at[slot, 0]).wait()
        for mine in range(2):
            pltpu.make_async_copy(
                rb.at[slot, whole], rb.at[slot, whole], sem.at[slot, 1 + mine]
            ).wait()

        def group(g, carry):
            done = []
            for q in range(GROUP):
                code = lst[g * GROUP + q]
                a = pl.multiple_of((code & 63) * BS, BS)
                b = pl.multiple_of(((code >> 6) & 63) * BS, BS)
                c = pl.multiple_of((code >> 12) * BS, BS)
                done.append((c, product(lb[slot, pl.ds(a, BS)], rb[slot, pl.ds(b, BS)])))
            for c, value in done:
                cb[pl.ds(c, BS)] += value
            return carry

        lax.fori_loop(0, (total + GROUP - 1) // GROUP, group, 0)
        return carry

    lax.fori_loop(0, count, panel, 0)
    store = pltpu.make_async_copy(cb.at[whole], out, sem.at[0, 3])
    store.start()
    store.wait()


def add_panels(stage, lefts, rights, before, depth, meta, kept, panels):
    arrays, numbers = [], {}

    def numbered(pieces):
        out = []
        for array, *rest in pieces:
            if id(array) not in numbers:
                numbers[id(array)] = len(arrays)
                arrays.append(array)
            out.append((numbers[id(array)], *rest))
        return out

    left_refs = {j: numbered(p) for j, p in lefts.items()}
    right_refs = {j: {k: numbered(p) for k, p in both.items()} for j, both in rights.items()}
    first = before is None
    body = functools.partial(panels_kernel, stage, left_refs, right_refs, first, len(arrays))
    smem = pl.BlockSpec(memory_space=pltpu.SMEM)
    hbm = pl.BlockSpec(memory_space=pl.ANY)
    args = arrays + ([] if first else [before])
    return pl.pallas_call(
        body,
        out_shape=jax.ShapeDtypeStruct((ROWS, BS), F32),
        in_specs=[smem] * 3 + [hbm] * len(args),
        out_specs=hbm,
        scratch_shapes=[
            pltpu.VMEM((2, ROWS, BS), F32),
            pltpu.VMEM((2, 2 * ROWS, BS), F32),
            pltpu.VMEM((ROWS + BS, BS), F32),
            pltpu.SMEM((2, EXTRA, BS), F32),
            pltpu.SMEM((2, 2, EXTRA, BS), F32),
            pltpu.SMEM((HALF * 16,), jnp.int32),
            pltpu.SMEM((HALF * SLOTS * SLOTS + GROUP,), jnp.int32),
            pltpu.SemaphoreType.DMA((2, 4)),
            pltpu.SemaphoreType.DMA((2, 3)),
        ],
        compiler_params=pltpu.CompilerParams(vmem_limit_bytes=16 << 20),
        cost_estimate=pl.CostEstimate(
            flops=panels * 400_000_000, bytes_accessed=panels * 5_000_000, transcendentals=0
        ),
    )(depth, meta, kept, *args)


def whole_piece(array):
    return [(array, 0, ROWS, 0, True)]


CUT = ROWS // 2


def half_pieces(front, back):
    return [(front, 0, CUT, 0, False), (back, 0, ROWS - CUT, CUT, True)]


def per_device(x_blocks, x_cols, c_cols):
    place = lax.axis_index(AXES)
    depth = lax.axis_index("depth").astype(jnp.int32).reshape(1)
    meta = lax.dynamic_index_in_dim(jnp.asarray(panel_table()), place, 0, keepdims=False)
    columns = jnp.pad(x_cols.reshape(1, HALF * SLOTS).astype(F32), ((0, EXTRA - 1), (0, BS - HALF * SLOTS)))
    own = jnp.concatenate([x_blocks.reshape(ROWS, BS), columns], 0)
    y1, y2 = move(own, y_flip=1), move(own, y_flip=2)
    swap = lambda value: move(value, d_flip=1)

    def ring(tile, axis):
        step = {axis: 1}, {axis: -1}
        behind, ahead = move(tile, **step[0]), move(tile, **step[1])
        front = move(behind[:CUT], **step[0])
        back = move(ahead[CUT:], **step[1])
        return [[tile], [behind], [ahead], [front, back]]

    def pieces(arrays):
        return whole_piece(arrays[0]) if len(arrays) == 1 else half_pieces(*arrays)

    left_sources = ring(own, "dz") + ring(y2, "dz")
    right_sources = ring(own, "dx") + ring(y1, "dx")
    lefts = {j: pieces(s) for j, s in enumerate(left_sources)}
    rights = {
        j: {
            (j, 0): pieces(s),
            (j, 1): pieces([swap(v) for v in s]),
        }
        for j, s in enumerate(right_sources)
    }
    meta = gate(gate(meta))
    total = None
    for stage, panels in enumerate((3, 3, 2)):
        there = [j for j in range(8) if STAGE[j] <= stage]
        total = add_panels(
            stage,
            {j: lefts[j] for j in there},
            {j: rights[j] for j in there},
            total,
            depth,
            meta,
            c_cols,
            panels,
        )
    return total.reshape(HALF, SLOTS, BS, BS)


def solution(mesh):
    return jax.shard_map(
        per_device,
        mesh=mesh,
        in_specs=(
            P(("row", "depth"), "col", None, None),
            P(("row", "depth"), "col"),
            P(("row", "depth"), "col"),
        ),
        out_specs=P(("row", "depth"), "col", None, None),
        check_vma=False,
    )
```

```python
import functools

import jax
import jax.numpy as jnp
import numpy as np
from jax import lax
from jax.experimental import pallas as pl
from jax.experimental.pallas import tpu as pltpu
from jax.sharding import PartitionSpec as P


AXES = ("row", "col", "depth")
RING = 4
HALF = 6
SLOTS = 4
BS = 128
ROWS = HALF * SLOTS * BS
EXTRA = 8
GROUP = 8
CUT = ROWS // 2
THIRD = ROWS // 3
TRASH = HALF * SLOTS
F32, BF16 = jnp.float32, jnp.bfloat16


def device_number(x, y, z, d):
    y_hi, y_lo = y >> 1, y & 1
    return (y_lo * RING + x) * 16 + (y_hi * RING + z) * 2 + d


def all_places():
    return [(x, y, z, d) for x in range(4) for y in range(4) for z in range(4) for d in range(2)]


def move(value, dx=0, dz=0, y_flip=0, d_flip=0):
    pairs = [
        (
            device_number(x, y, z, d),
            device_number(
                (x + dx * (1 - 2 * d)) % 4, y ^ y_flip, (z + dz * (1 - 2 * d)) % 4, d ^ d_flip
            ),
        )
        for x, y, z, d in all_places()
    ]
    return lax.ppermute(value, AXES, pairs)


LEFT_STAGE = (0, 0, 1, 2, 1, 2, 6, 7)
RIGHT_STAGE = (0, 0, 1, 2, 3, 4, 8, 4, 8, 5)
STAGES = 9
WIDTH = 18


def panel_table():
    table = np.zeros((128, STAGES, WIDTH), np.int32)
    for x, y, z, d in all_places():
        rows = table[device_number(x, y, z, d)]
        rows[:, WIDTH - 1] = d
        place = (0, 1, 3, 2) if d else (0, 2, 3, 1)
        for h in range(2):
            for w in range(4):
                left = 4 * (h != y >> 1) + place[(w - z) % 4]
                right = place[(w - x) % 4]
                for source in [(right,), ((4,), (5, 6), (7, 8), (9,))[right]][h != (y & 1)]:
                    row = rows[max(LEFT_STAGE[left], RIGHT_STAGE[source])]
                    row[1 + 2 * row[0]] = left
                    row[2 + 2 * row[0]] = source
                    row[0] += 1
    return table


def split(value):
    high = value.astype(BF16)
    return high, (value - high.astype(F32)).astype(BF16)


def product(a, b):
    a_high, a_low = split(a)
    b_high, b_low = split(b)
    side = jnp.concatenate([b_high, b_low], 1)
    both = jnp.dot(
        jnp.concatenate([a_high, a_low], 1),
        jnp.concatenate([side, side], 0),
        preferred_element_type=F32,
    )
    return both[:, :BS] + both[:, BS:]


def table_kernel(meta_ref, kept_ref, o_ref):
    for i in range(STAGES):
        for j in range(WIDTH):
            o_ref[i, j] = meta_ref[i, j]
    for i in range(HALF):
        for u in range(SLOTS):
            o_ref[STAGES + i, u] = kept_ref[i, u]


def gate_kernel(a_ref, o_ref):
    for i in range(STAGES):
        for j in range(WIDTH):
            o_ref[i, j] = a_ref[i, j]
    for i in range(HALF):
        for u in range(SLOTS):
            o_ref[STAGES + i, u] = a_ref[STAGES + i, u]


def gate(body, *args):
    return pl.pallas_call(
        body,
        out_shape=jax.ShapeDtypeStruct((STAGES + HALF, WIDTH), jnp.int32),
        in_specs=[pl.BlockSpec(memory_space=pltpu.SMEM)] * len(args),
        out_specs=pl.BlockSpec(memory_space=pltpu.SMEM),
        cost_estimate=pl.CostEstimate(flops=100, bytes_accessed=1000, transcendentals=0),
    )(*args)


def panels_kernel(stage, lefts, rights, n_refs, meta_ref, *refs):
    first, last = stage == 0, stage == STAGES - 1
    pieces = refs[:n_refs]
    at = n_refs if first else n_refs + 1
    out, lb, rb, lc, rc, inv, lst, sem, csem = refs[at : at + 9]
    cb = refs[at + 9] if last else out
    depth = meta_ref[0, WIDTH - 1]
    count = meta_ref[stage, 0]
    whole = pl.ds(0, ROWS)

    def copies(j, sources, dst, cols, data_sem, col_sem):
        for ref, src, rows, to, has_cols in sources[j]:
            pltpu.make_async_copy(
                pieces[ref].at[pl.ds(src, rows)], dst.at[pl.ds(to, rows)], data_sem
            ).start()
            if has_cols:
                pltpu.make_async_copy(
                    pieces[ref].at[pl.ds(src + rows, EXTRA)], cols, col_sem
                ).start()

    def fetch(n, slot):
        left, right = meta_ref[stage, 1 + 2 * n], meta_ref[stage, 2 + 2 * n]
        for j in lefts:
            @pl.when(left == j)
            def _():
                copies(j, lefts, lb.at[slot], lc.at[slot], sem.at[slot, 0], csem.at[slot, 0])
        for j in rights:
            @pl.when(right == j)
            def _():
                for mine in range(2):
                    half = depth if mine == 0 else 1 - depth
                    copies(
                        (j, mine),
                        rights[j],
                        rb.at[slot, pl.ds(pl.multiple_of(half * ROWS, ROWS), ROWS)],
                        rc.at[slot, half],
                        sem.at[slot, 1 + mine],
                        csem.at[slot, 1 + mine],
                    )

    @pl.when(count > 0)
    def _():
        fetch(0, 0)

    if first:
        cb[...] = jnp.zeros_like(cb)
    else:
        cb[...] = refs[n_refs][...]

    @pl.when(count > 0)
    def _():
        def clear(n, carry):
            inv[n] = -1
            return carry

        lax.fori_loop(0, HALF * 16, clear, 0)
        for i in range(HALF):
            for u in range(SLOTS):
                inv[i * 16 + meta_ref[STAGES + i, u]] = u

    def panel(n, carry):
        slot = lax.rem(n, 2)
        source = meta_ref[stage, 2 + 2 * n]
        part = jnp.where(jnp.logical_or(source < 5, source > 8), 2, (source + 1) & 1)
        low = jnp.where(part == 1, HALF // 2, 0)
        high = jnp.where(part == 0, HALF // 2, HALF)

        @pl.when(n + 1 < count)
        def _():
            fetch(n + 1, 1 - slot)

        pltpu.make_async_copy(lc.at[slot], lc.at[slot], csem.at[slot, 0]).wait()
        for mine in range(2):
            pltpu.make_async_copy(rc.at[slot, 0], rc.at[slot, 0], csem.at[slot, 1 + mine]).wait()

        def list_row(e, total):
            i = e // SLOTS
            k = lc[slot, 0, e].astype(jnp.int32)
            half = (k >= HALF).astype(jnp.int32)
            within = k - HALF * half
            there = jnp.logical_and(within >= low, within < high).astype(jnp.int32)
            base = within * SLOTS
            code = e + k * 256
            for t in range(SLOTS):
                column = rc[slot, half, 0, base + t].astype(jnp.int32)
                u = inv[i * 16 + column]
                lst[total] = code + t * 64 + (i * SLOTS + u) * 4096
                total = total + jnp.where(u >= 0, there, 0)
            return total

        total = lax.fori_loop(0, HALF * SLOTS, list_row, 0)
        for q in range(GROUP):
            lst[total + q] = TRASH * 4096
        pltpu.make_async_copy(lb.at[slot], lb.at[slot], sem.at[slot, 0]).wait()
        for rows, when in ((ROWS, part == 2), (CUT, part < 2)):
            @pl.when(when)
            def _():
                for mine in range(2):
                    view = rb.at[slot, pl.ds(0, rows)]
                    pltpu.make_async_copy(view, view, sem.at[slot, 1 + mine]).wait()

        def group(g, carry):
            done = []
            for q in range(GROUP):
                code = lst[g * GROUP + q]
                a = pl.multiple_of((code & 63) * BS, BS)
                b = pl.multiple_of(((code >> 6) & 63) * BS, BS)
                c = pl.multiple_of((code >> 12) * BS, BS)
                done.append((c, product(lb[slot, pl.ds(a, BS)], rb[slot, pl.ds(b, BS)])))
            for c, value in done:
                cb[pl.ds(c, BS)] += value
            return carry

        lax.fori_loop(0, (total + GROUP - 1) // GROUP, group, 0)
        return carry

    lax.fori_loop(0, count, panel, 0)
    if last:
        store = pltpu.make_async_copy(cb.at[whole], out, sem.at[0, 3])
        store.start()
        store.wait()


def add_panels(stage, lefts, rights, before, meta, panels):
    arrays, numbers = [], {}

    def numbered(pieces):
        out = []
        for array, *rest in pieces:
            if id(array) not in numbers:
                numbers[id(array)] = len(arrays)
                arrays.append(array)
            out.append((numbers[id(array)], *rest))
        return out

    left_refs = {j: numbered(p) for j, p in lefts.items()}
    right_refs = {j: {k: numbered(p) for k, p in both.items()} for j, both in rights.items()}
    body = functools.partial(panels_kernel, stage, left_refs, right_refs, len(arrays))
    smem = pl.BlockSpec(memory_space=pltpu.SMEM)
    hbm = pl.BlockSpec(memory_space=pl.ANY)
    vmem = pl.BlockSpec(memory_space=pltpu.VMEM)
    first, last = stage == 0, stage == STAGES - 1
    args = arrays + ([] if first else [before])
    return pl.pallas_call(
        body,
        out_shape=jax.ShapeDtypeStruct((ROWS if last else ROWS + BS, BS), F32),
        in_specs=[smem] + [hbm] * len(arrays) + [vmem] * (not first),
        out_specs=hbm if last else vmem,
        input_output_aliases={} if first or last else {1 + len(arrays): 0},
        scratch_shapes=[
            pltpu.VMEM((2, ROWS, BS), F32),
            pltpu.VMEM((2, 2 * ROWS, BS), F32),
            pltpu.SMEM((2, EXTRA, BS), F32),
            pltpu.SMEM((2, 2, EXTRA, BS), F32),
            pltpu.SMEM((HALF * 16,), jnp.int32),
            pltpu.SMEM((HALF * SLOTS * SLOTS + GROUP,), jnp.int32),
            pltpu.SemaphoreType.DMA((2, 4)),
            pltpu.SemaphoreType.DMA((2, 3)),
        ]
        + [pltpu.VMEM((ROWS + BS, BS), F32)] * last,
        compiler_params=pltpu.CompilerParams(vmem_limit_bytes=16 << 20),
        cost_estimate=pl.CostEstimate(
            flops=panels * 400_000_000, bytes_accessed=panels * 5_000_000, transcendentals=0
        ),
    )(meta, *args)


def pieces(*arrays):
    out, at = [], 0
    for n, (array, rows) in enumerate(arrays):
        out.append((array, 0, rows, at, n == len(arrays) - 1))
        at += rows
    return out


def per_device(x_blocks, x_cols, c_cols):
    columns = jnp.pad(
        x_cols.reshape(1, HALF * SLOTS).astype(F32), ((0, EXTRA - 1), (0, BS - HALF * SLOTS))
    )
    blocks = x_blocks.reshape(ROWS, BS)
    own = jnp.concatenate([blocks, columns], 0)
    own_a, own_b = jnp.concatenate([blocks[:CUT], columns], 0), own[CUT:]
    place = lax.axis_index(AXES)
    meta = lax.dynamic_index_in_dim(jnp.asarray(panel_table()), place, 0, keepdims=False)

    def swap(value):
        return move(value, d_flip=1)

    other = swap(own)
    z1, z2 = move(own, dz=1), move(other, dz=1)
    x1, x2 = move(own, dx=1), move(other, dx=1)
    z3, x3 = move(z1, dz=1), move(x1, dx=1)
    left = move(own, y_flip=2)
    ya, yb = move(own_a, y_flip=1), move(own_b, y_flip=1)
    sa, sb = swap(ya), swap(yb)
    Z1, Z2 = move(left, dz=1), move(swap(left), dz=1)
    X1, X2 = move(ya, dx=1), move(sa, dx=1)
    U1, U2 = move(yb, dx=1), move(sb, dx=1)
    ez, Z3 = move(z3[:THIRD], y_flip=2), move(Z1[THIRD:], dz=1)
    ex, X3 = move(x3[CUT:], y_flip=1), move(X1, dx=1)
    left_arrays = ((own,), (z1,), (swap(z2),), (z3,), (left,), (Z1,), (swap(Z2),), (ez, Z3))
    right_arrays = (
        ((own,), (other,)),
        ((x1,), (x2,)),
        ((swap(x2),), (swap(x1),)),
        ((x3,), (swap(x3),)),
        ((ya, yb), (sa, sb)),
        ((X1,), (X2,)),
        ((U1,), (U2,)),
        ((swap(X2),), (swap(X1),)),
        ((swap(U2),), (swap(U1),)),
        ((X3, ex), (swap(X3), swap(ex))),
    )

    def right_pieces(arrays, j):
        if len(arrays) == 2:
            return pieces(*((v, CUT) for v in arrays))
        if j < 4:
            return pieces((arrays[0], ROWS))
        return [(arrays[0], 0, CUT, CUT * (j in (6, 8)), True)]

    lefts = {
        j: pieces(*((v, min(v.shape[0], ROWS) - EXTRA * (v is Z3)) for v in arrays))
        for j, arrays in enumerate(left_arrays)
    }
    rights = {
        j: {(j, mine): right_pieces(v, j) for mine, v in enumerate(both)}
        for j, both in enumerate(right_arrays)
    }
    meta = gate(gate_kernel, gate(table_kernel, meta, c_cols))
    total = None
    for stage in range(STAGES):
        total = add_panels(
            stage,
            {j: v for j, v in lefts.items() if LEFT_STAGE[j] <= stage},
            {j: v for j, v in rights.items() if RIGHT_STAGE[j] <= stage},
            total,
            meta,
            1,
        )
    return total.reshape(HALF, SLOTS, BS, BS)


def solution(mesh):
    return jax.shard_map(
        per_device,
        mesh=mesh,
        in_specs=(
            P(("row", "depth"), "col", None, None),
            P(("row", "depth"), "col"),
            P(("row", "depth"), "col"),
        ),
        out_specs=P(("row", "depth"), "col", None, None),
        check_vma=False,
    )
```

```python
import functools

import jax
import jax.numpy as jnp
import numpy as np
from jax import lax
from jax.experimental import pallas as pl
from jax.experimental.pallas import tpu as pltpu
from jax.sharding import PartitionSpec as P


AXES = ("row", "col", "depth")
RING = 4
HALF = 6
SLOTS = 4
BS = 128
ROWS = HALF * SLOTS * BS
EXTRA = 8
GROUP = 16
CUT = ROWS // 2
THIRD = ROWS // 3
TRASH = HALF * SLOTS
F32, BF16 = jnp.float32, jnp.bfloat16


def device_number(x, y, z, d):
    y_hi, y_lo = y >> 1, y & 1
    return (y_lo * RING + x) * 16 + (y_hi * RING + z) * 2 + d


def all_places():
    return [(x, y, z, d) for x in range(4) for y in range(4) for z in range(4) for d in range(2)]


def move(value, dx=0, dz=0, y_flip=0, d_flip=0):
    pairs = [
        (
            device_number(x, y, z, d),
            device_number(
                (x + dx * (1 - 2 * d)) % 4, y ^ y_flip, (z + dz * (1 - 2 * d)) % 4, d ^ d_flip
            ),
        )
        for x, y, z, d in all_places()
    ]
    return lax.ppermute(value, AXES, pairs)


LEFT_STAGE = (0, 0, 1, 2, 1, 1, 6, 7)
RIGHT_STAGE = (0, 0, 1, 1, 3, 4, 7, 4, 7, 5)
MOST = (2, 1, 1, 1, 2, 1, 1, 3)
STAGES = len(MOST)
WIDTH = 18


def panel_table():
    table = np.zeros((128, STAGES, WIDTH), np.int32)
    for x, y, z, d in all_places():
        rows = table[device_number(x, y, z, d)]
        rows[:, WIDTH - 1] = d
        place = (0, 1, 3, 2) if d else (0, 2, 3, 1)
        pairs = []
        for h in range(2):
            for w in range(4):
                left = 4 * (h != y >> 1) + place[(w - z) % 4]
                right = place[(w - x) % 4]
                for source in [(right,), ((4,), (5, 6), (7, 8), (9,))[right]][h != (y & 1)]:
                    there = max(LEFT_STAGE[left], RIGHT_STAGE[source])
                    pairs.append((there, source not in (5, 6, 7, 8), left, source))
        for stage, most in enumerate(MOST):
            now = sorted(p for p in pairs if p[0] <= stage)[:most]
            pairs = [p for p in pairs if p not in now]
            rows[stage, 0] = len(now)
            for n, (_, _, left, source) in enumerate(now):
                rows[stage, 1 + 2 * n : 3 + 2 * n] = left, source
        assert not pairs
    return table


def split(value):
    high = value.astype(BF16)
    return high, (value - high.astype(F32)).astype(BF16)


def product(a, b):
    a_high, a_low = split(a)
    b_high, b_low = split(b)
    side = jnp.concatenate([b_high, b_low], 1)
    both = jnp.dot(
        jnp.concatenate([a_high, a_low], 1),
        jnp.concatenate([side, side], 0),
        preferred_element_type=F32,
    )
    return both[:, :BS] + both[:, BS:]


def table_kernel(meta_ref, kept_ref, o_ref):
    for i in range(STAGES):
        for j in range(WIDTH):
            o_ref[i, j] = meta_ref[i, j]
    for i in range(HALF):
        for column in range(2 * HALF):
            o_ref[STAGES + i, column] = -1
        for u in range(SLOTS):
            o_ref[STAGES + i, kept_ref[i, u]] = (i * SLOTS + u) * 65536


def gate_kernel(a_ref, o_ref):
    for i in range(STAGES):
        for j in range(WIDTH):
            o_ref[i, j] = a_ref[i, j]
    for i in range(HALF):
        for column in range(2 * HALF):
            o_ref[STAGES + i, column] = a_ref[STAGES + i, column]


def gate(body, *args):
    return pl.pallas_call(
        body,
        out_shape=jax.ShapeDtypeStruct((STAGES + HALF, WIDTH), jnp.int32),
        in_specs=[pl.BlockSpec(memory_space=pltpu.SMEM)] * len(args),
        out_specs=pl.BlockSpec(memory_space=pltpu.SMEM),
        cost_estimate=pl.CostEstimate(flops=100, bytes_accessed=1000, transcendentals=0),
    )(*args)


def panels_kernel(stage, entries, lefts, rights, n_refs, meta_ref, *refs):
    first, last = stage == 0, stage == STAGES - 1
    pieces = refs[:n_refs]
    at = n_refs if first else n_refs + 1
    out, lb, rb, lc, rc, lst, starts, sem, csem, lsem = refs[at : at + 10]
    cb = refs[at + 10] if last else out
    parts = any(j in rights for j in (5, 6, 7, 8))
    depth = meta_ref[0, WIDTH - 1]
    count = meta_ref[stage, 0]

    def copies(sources, dst, data_sem, cols, col_sem):
        for ref, src, rows, to, has_cols in sources:
            if has_cols:
                pltpu.make_async_copy(
                    pieces[ref].at[pl.ds(src + rows, EXTRA)], cols, col_sem
                ).start()
            pltpu.make_async_copy(
                pieces[ref].at[pl.ds(src, rows)], dst.at[pl.ds(to, rows)], data_sem
            ).start()

    def fetch(n, carry):
        left, right = meta_ref[stage, 1 + 2 * n], meta_ref[stage, 2 + 2 * n]
        for j in lefts:
            @pl.when(left == j)
            def _():
                dst = lb.at[pl.ds(pl.multiple_of(n * ROWS, ROWS), ROWS)]
                copies(lefts[j], dst, sem.at[n, 0], lc.at[n], csem.at[n, 0])
        for j in rights:
            @pl.when(right == j)
            def _():
                for mine in range(2):
                    half = depth if mine == 0 else 1 - depth
                    dst = rb.at[pl.ds(pl.multiple_of((2 * n + half) * ROWS, ROWS), ROWS)]
                    copies(
                        rights[j][j, mine],
                        dst,
                        sem.at[n, 1 + mine],
                        rc.at[n, half],
                        csem.at[n, 1 + mine],
                    )
        return carry

    def part_of(n):
        source = meta_ref[stage, 2 + 2 * n]
        return jnp.where(jnp.logical_or(source < 5, source > 8), 2, (source + 1) & 1)

    def arrive(n):
        view = lb.at[pl.ds(0, ROWS)]
        pltpu.make_async_copy(view, view, sem.at[n, 0]).wait()
        for rows, when in ((ROWS, part_of(n) == 2), (CUT, part_of(n) < 2)):
            @pl.when(when)
            def _():
                for mine in range(2):
                    view = rb.at[pl.ds(0, rows)]
                    pltpu.make_async_copy(view, view, sem.at[n, 1 + mine]).wait()

    @pl.when(count > 0)
    def _():
        lax.fori_loop(0, count, fetch, 0)

    if first:
        cb[...] = jnp.zeros_like(cb)
    else:
        load = pltpu.make_async_copy(refs[n_refs], cb, lsem.at[0])
        load.start()

    def list_panel(n, total):
        starts[n] = total
        a_first = n * (HALF * SLOTS) + n * (2 * HALF * SLOTS * 256)
        low = jnp.where(part_of(n) == 1, HALF // 2, 0)
        high = jnp.where(part_of(n) == 0, HALF // 2, HALF)
        pltpu.make_async_copy(lc.at[n], lc.at[n], csem.at[n, 0]).wait()
        for mine in range(2):
            pltpu.make_async_copy(rc.at[n, 0], rc.at[n, 0], csem.at[n, 1 + mine]).wait()

        def list_row(i, total):
            found = []
            for s in range(SLOTS):
                k = lc[n, 0, i * SLOTS + s].astype(jnp.int32)
                half = (k >= HALF).astype(jnp.int32)
                within = k - HALF * half
                code = a_first + i * SLOTS + s + k * (SLOTS * 256)
                there = 1
                if parts:
                    there = jnp.logical_and(within >= low, within < high).astype(jnp.int32)
                for t in range(SLOTS):
                    column = rc[n, half, 0, within * SLOTS + t].astype(jnp.int32)
                    place = meta_ref[STAGES + i, column]
                    found.append((code + t * 256 + place, ((place >> 31) + 1) * there))
            for code, kept in found:
                lst[total] = code
                total = total + kept
            return total

        return lax.fori_loop(0, HALF, list_row, total)

    total = lax.fori_loop(0, count, list_panel, 0)
    if not first:
        load.wait()
    for q in range(GROUP):
        lst[total + q] = TRASH * 65536
    groups = (total + GROUP - 1) // GROUP

    def arrivals(below, beyond):
        for n in range(entries):
            @pl.when(n < count)
            def _():
                @pl.when((starts[n] >= below) & (starts[n] < beyond))
                def _():
                    arrive(n)

    def group(g, carry):
        arrivals(g * GROUP, (g + 1) * GROUP)
        done = []
        for q in range(GROUP):
            code = lst[g * GROUP + q]
            a = pl.multiple_of((code & 255) * BS, BS)
            b = pl.multiple_of(((code >> 8) & 255) * BS, BS)
            c = pl.multiple_of((code >> 16) * BS, BS)
            done.append((c, product(lb[pl.ds(a, BS)], rb[pl.ds(b, BS)])))
        for c, value in done:
            cb[pl.ds(c, BS)] += value
        return carry

    lax.fori_loop(0, groups, group, 0)
    arrivals(groups * GROUP, entries * HALF * SLOTS * SLOTS + 1)
    if last:
        store = pltpu.make_async_copy(cb.at[pl.ds(0, ROWS)], out, lsem.at[0])
        store.start()
        store.wait()


def add_panels(stage, entries, lefts, rights, before, meta, panels):
    arrays, numbers = [], {}

    def numbered(pieces):
        out = []
        for array, *rest in pieces:
            if id(array) not in numbers:
                numbers[id(array)] = len(arrays)
                arrays.append(array)
            out.append((numbers[id(array)], *rest))
        return out

    left_refs = {j: numbered(p) for j, p in lefts.items()}
    right_refs = {j: {k: numbered(p) for k, p in both.items()} for j, both in rights.items()}
    body = functools.partial(panels_kernel, stage, entries, left_refs, right_refs, len(arrays))
    smem = pl.BlockSpec(memory_space=pltpu.SMEM)
    hbm = pl.BlockSpec(memory_space=pl.ANY)
    vmem = pl.BlockSpec(memory_space=pltpu.VMEM)
    first, last = stage == 0, stage == STAGES - 1
    args = arrays + ([] if first else [before])
    return pl.pallas_call(
        body,
        out_shape=jax.ShapeDtypeStruct((ROWS if last else ROWS + BS, BS), F32),
        in_specs=[smem] + [hbm] * len(arrays) + [vmem] * (not first),
        out_specs=hbm if last else vmem,
        scratch_shapes=[
            pltpu.VMEM((entries * ROWS, BS), F32),
            pltpu.VMEM((entries * 2 * ROWS, BS), F32),
            pltpu.SMEM((entries, EXTRA, BS), F32),
            pltpu.SMEM((entries, 2, EXTRA, BS), F32),
            pltpu.SMEM((entries * HALF * SLOTS * SLOTS + GROUP,), jnp.int32),
            pltpu.SMEM((entries,), jnp.int32),
            pltpu.SemaphoreType.DMA((entries, 3)),
            pltpu.SemaphoreType.DMA((entries, 3)),
            pltpu.SemaphoreType.DMA((1,)),
        ]
        + [pltpu.VMEM((ROWS + BS, BS), F32)] * last,
        compiler_params=pltpu.CompilerParams(
            vmem_limit_bytes=(9 * entries + 3 + 4 * last) << 19),
        cost_estimate=pl.CostEstimate(
            flops=panels * 400_000_000, bytes_accessed=panels * 5_000_000, transcendentals=0
        ),
    )(meta, *args)


def pieces(*arrays):
    out, at = [], 0
    for n, (array, rows) in enumerate(arrays):
        out.append((array, 0, rows, at, n == len(arrays) - 1))
        at += rows
    return out


def per_device(x_blocks, x_cols, c_cols):
    columns = jnp.pad(
        x_cols.reshape(1, HALF * SLOTS).astype(F32), ((0, EXTRA - 1), (0, BS - HALF * SLOTS))
    )
    blocks = x_blocks.reshape(ROWS, BS)
    own = jnp.concatenate([blocks, columns], 0)
    own_a, own_b = jnp.concatenate([blocks[:CUT], columns], 0), own[CUT:]
    place = lax.axis_index(AXES)
    meta = lax.dynamic_index_in_dim(jnp.asarray(panel_table()), place, 0, keepdims=False)

    def swap(value):
        return move(value, d_flip=1)

    other = swap(own)
    z1, z2 = move(own, dz=1), move(other, dz=1)
    x1, x2 = move(own, dx=1), move(other, dx=1)
    z3, x3 = move(z1, dz=1), move(x1, dx=1)
    left = move(own, y_flip=2)
    ya, yb = move(own_a, y_flip=1), move(own_b, y_flip=1)
    sa, sb = swap(ya), swap(yb)
    Z1, Z2 = move(left, dz=1), move(swap(left), dz=1)
    X1, X2 = move(ya, dx=1), move(sa, dx=1)
    U1, U2 = move(yb, dx=1), move(sb, dx=1)
    ez, Z3 = move(z3[:THIRD], y_flip=2), move(Z1[THIRD:], dz=1)
    ex, X3 = move(x3[CUT:], y_flip=1), move(X1, dx=1)
    left_arrays = ((own,), (z1,), (swap(z2),), (z3,), (left,), (Z1,), (swap(Z2),), (ez, Z3))
    right_arrays = (
        ((own,), (other,)),
        ((x1,), (x2,)),
        ((swap(x2),), (swap(x1),)),
        ((x3,), (swap(x3),)),
        ((ya, yb), (sa, sb)),
        ((X1,), (X2,)),
        ((U1,), (U2,)),
        ((swap(X2),), (swap(X1),)),
        ((swap(U2),), (swap(U1),)),
        ((X3, ex), (swap(X3), swap(ex))),
    )

    def right_pieces(arrays, j):
        if len(arrays) == 2:
            return pieces(*((v, CUT) for v in arrays))
        if j < 4:
            return pieces((arrays[0], ROWS))
        return [(arrays[0], 0, CUT, CUT * (j in (6, 8)), True)]

    lefts = {
        j: pieces(*((v, min(v.shape[0], ROWS) - EXTRA * (v is Z3)) for v in arrays))
        for j, arrays in enumerate(left_arrays)
    }
    rights = {
        j: {(j, mine): right_pieces(v, j) for mine, v in enumerate(both)}
        for j, both in enumerate(right_arrays)
    }
    meta = gate(gate_kernel, gate(table_kernel, meta, c_cols))
    table = panel_table()
    used = [
        tuple({row[n] for row in table[:, stage] for n in range(1 + side, 1 + 2 * row[0], 2)} for side in range(2))
        for stage in range(STAGES)
    ]
    total = None
    for stage in range(STAGES):
        total = add_panels(
            stage,
            int(table[:, stage, 0].max()),
            {j: v for j, v in lefts.items() if j in used[stage][0]},
            {j: v for j, v in rights.items() if j in used[stage][1]},
            total,
            meta,
            1,
        )
    return total.reshape(HALF, SLOTS, BS, BS)


def solution(mesh):
    return jax.shard_map(
        per_device,
        mesh=mesh,
        in_specs=(
            P(("row", "depth"), "col", None, None),
            P(("row", "depth"), "col"),
            P(("row", "depth"), "col"),
        ),
        out_specs=P(("row", "depth"), "col", None, None),
        check_vma=False,
    )
```
